512 devices in a mesh: ctx: 64 (over z, x), head: 8 (over y, core).
Axes of the slice: x: 4, y: 4, z: 16, core: 2. Of those that a mesh axis runs over, the one named last changes fastest.
Arguments:
- queries: bfloat16 [8192, 8192], P('ctx', 'head'), may hold values from -6 to 6
- key_rows: bfloat16 [8192, 8192], P('ctx', 'head'), may hold values from -0.5 to 0.5
- value_rows: bfloat16 [8192, 8192], P('ctx', 'head'), may hold values from -40 to 40
- log_decay: float32 [8192, 64], P('ctx', 'head'), may hold values from -1.5 to 0
- doc_start: int32 [128], P('ctx'), may hold values from 0 to 64, as said below
- out_cotangent: bfloat16 [8192, 8192], P('ctx', 'head'), may hold values from -6 to 6
Outputs:
- query_grad: bfloat16 [8192, 8192], P('ctx', 'head')
- key_grad: bfloat16 [8192, 8192], P('ctx', 'head')
- value_grad: bfloat16 [8192, 8192], P('ctx', 'head')
The draws below stay inside these ranges and needn't reach their ends.
Inputs may be any that keep to these rules, and one draw needn't show every extreme that they name: `doc_start`: entry b is the offset within rows b * 64 to (b + 1) * 64 - 1 at which a new document begins, 64 where none begins. The first entry is 0 and the last is 64.
All inputs are finite; a program needn't handle non-finite values.
Results may differ from the reference program's by a relative error of at most 0.0069.
Values sent between devices are 32-bit elements; how exact they have to be, the bound alone decides.
A program may use at most 128 MiB of HBM per device.

```python
import math
import jax
import jax.numpy as jnp
from jax import lax

DH = 128
TOK_DEV = 128
BLK = 64
HEAD_TOTAL = 64
F = 8192
SEQUENCE_LENGTH = 8192
NBLK = 128
N_CTX = 64


def draw_value_rows(key, part):
    random_subkeys = jax.random.split(key, 2)
    head_place = (jnp.arange(F) // DH).astype(jnp.float32) / max(HEAD_TOTAL - 1, 1)
    column_scale = 10.0 ** head_place
    row_scale = 10.0 ** jax.random.uniform(random_subkeys[1], (SEQUENCE_LENGTH, 1), minval=0.0, maxval=1.0)
    base_draw = jnp.clip(jax.random.normal(random_subkeys[0], (SEQUENCE_LENGTH, F)), -4.0, 4.0)
    return (0.1 * base_draw * column_scale[None, :] * row_scale).astype(jnp.bfloat16)


def draw_log_decay(key, part):
    random_subkeys = jax.random.split(key, 8)
    span_count = SEQUENCE_LENGTH // TOK_DEV
    fast_limit = 4
    fast_heads = jax.random.randint(random_subkeys[0], (1, 1, HEAD_TOTAL), 0, 8) < fast_limit
    fast_rate = 1.0 / jax.random.uniform(random_subkeys[1], (1, 1, HEAD_TOTAL), minval=30.0, maxval=50.0)
    span_factor = jnp.exp(jax.random.uniform(random_subkeys[2], (span_count, 1, HEAD_TOTAL), minval=0.0, maxval=math.log(2.5)))
    light_loss = 0.4 / span_count * span_factor
    heavy_spans = jax.random.randint(random_subkeys[6], (1, 3, HEAD_TOTAL), 0, span_count)
    span_index = jnp.arange(span_count)[:, None, None]
    heavy = jnp.any(span_index == heavy_spans, axis=1)[:, None, :]
    heavy_loss = jax.random.uniform(random_subkeys[7], (span_count, 1, HEAD_TOTAL), minval=0.2, maxval=0.3)
    slow_token = jnp.where(heavy, heavy_loss, light_loss) / TOK_DEV
    fast_token = fast_rate * span_factor
    token_wise = jnp.where(fast_heads, fast_token, slow_token)
    token_wise = jnp.broadcast_to(token_wise, (span_count, TOK_DEV, HEAD_TOTAL)).reshape(SEQUENCE_LENGTH, HEAD_TOTAL)
    jaggedness = jax.random.uniform(random_subkeys[3], (SEQUENCE_LENGTH, HEAD_TOTAL), minval=0.5, maxval=1.5)
    segment_block_rows = jax.random.randint(random_subkeys[4], (2,), 0, SEQUENCE_LENGTH)
    segment_width = jnp.log(jax.random.uniform(random_subkeys[5], (2, HEAD_TOTAL), minval=0.7, maxval=0.8))
    row_position_index = jnp.arange(SEQUENCE_LENGTH)[:, None]
    segment_blocks = (row_position_index == segment_block_rows[0]) * segment_width[0][None, :] + (row_position_index == segment_block_rows[1]) * segment_width[1][None, :]
    return (segment_blocks - token_wise * jaggedness).astype(jnp.float32)


def draw_doc_start(key, part):
    random_subkeys = jax.random.split(key, 2)
    chance = jax.random.randint(random_subkeys[0], (NBLK,), 0, NBLK)
    offset = jax.random.randint(random_subkeys[1], (NBLK,), 0, BLK)
    starts = jnp.where(chance < 4, offset, BLK)
    block_index = jnp.arange(NBLK)
    starts = jnp.where(block_index == 0, 0, starts)
    starts = jnp.where(block_index == NBLK - 1, BLK, starts)
    return starts.astype(jnp.int32)


def level_of(own_key, extent, cuts, smallest, high):
    factor_of, own = 1.0, jax.random.fold_in(own_key, 6)
    for position, blocks in cuts:
        draws = jnp.exp(jax.random.uniform(jax.random.fold_in(own, position), (blocks,), jnp.float32, smallest / len(cuts), high / len(cuts)))
        factor_of = factor_of * jnp.repeat(draws, extent[position] // blocks).reshape([-1 if axis == position else 1 for axis in range(len(extent))])
    return factor_of


def noise(key, dims, scale, most, shards=(), dtype=jnp.bfloat16):
    factor_of = level_of(key, dims, shards, -0.22, 0.18) if shards else 1.0
    result = jax.random.normal(key, dims, jnp.float32) * scale * factor_of
    return jnp.minimum(jnp.maximum(result, -most), most).astype(dtype)


def setup_inputs(seed: int = 0) -> dict:
    key_of = jax.random.split(jax.random.key(seed), 7)
    queries = noise(key_of[0], (SEQUENCE_LENGTH, F), 1.0, 6.0, ((0, 64), (1, 8)))
    key_rows = noise(key_of[1], (SEQUENCE_LENGTH, F), DH ** -0.5, 0.5, ((0, 64), (1, 8)))
    value_rows = draw_value_rows(jax.random.fold_in(key_of[6], 71), 0)
    log_decay = draw_log_decay(jax.random.fold_in(key_of[6], 71), 0)
    doc_start = draw_doc_start(jax.random.fold_in(key_of[6], 71), 0)
    out_cotangent = noise(key_of[5], (SEQUENCE_LENGTH, F), 1.0, 6.0, ((0, 64), (1, 8)))
    return {"queries": queries, "key_rows": key_rows, "value_rows": value_rows, "log_decay": log_decay, "doc_start": doc_start, "out_cotangent": out_cotangent}


epsilon = 1e-05

def product(form, left, right):
    return jnp.einsum(form, left.astype(jnp.float32), right.astype(jnp.float32), precision=lax.Precision.HIGHEST)

def decay_terms(log_decay, doc_start):
    row_count = log_decay.shape[0]
    block_rows = row_count // doc_start.shape[0]
    row_position_index = lax.broadcasted_iota(jnp.int32, (row_count, 1), 0)
    block_index = lax.broadcasted_iota(jnp.int32, (1, doc_start.shape[0]), 1)
    reset_rows = jnp.where(doc_start[None, :] < block_rows, block_index * block_rows + doc_start[None, :], -1)
    reset_flag = lax.optimization_barrier(jnp.sum((row_position_index == reset_rows).astype(jnp.int32), axis=1))
    segment = jnp.cumsum(reset_flag)
    cumulative = jnp.cumsum(log_decay, axis=0)
    carried_in = jnp.where((segment == 0)[:, None], jnp.exp(cumulative), 0.0)
    to_end = jnp.where((segment == segment[-1])[:, None], jnp.exp(cumulative[-1][None, :] - cumulative), 0.0)
    causal = (row_position_index >= row_position_index.T) & (segment[:, None] == segment[None, :])
    log_gap = cumulative.T[:, :, None] - cumulative.T[:, None, :]
    within = jnp.where(causal[None], jnp.exp(jnp.where(causal[None], log_gap, 0.0)), 0.0)
    return (carried_in, to_end, within)

def chain_combine(earlier, latter):
    return (earlier[0] * latter[0], latter[0][..., None, None] * earlier[1] + latter[1])

def forward_local(queries, key_rows, value_rows, to_end, within):
    scores = product('thd,shd->hts', queries, key_rows)
    weights = (scores * within).astype(jnp.bfloat16)
    within_out = product('hts,shd->thd', weights, value_rows)
    weighted_keys = (key_rows * to_end[:, :, None]).astype(jnp.bfloat16)
    end_state = product('shd,she->hde', weighted_keys, value_rows)
    return (weights, within_out, weighted_keys, end_state)

def norm_backward(flat_out, out_grad, sum_squares, sum_cross, feature_total):
    inv_rms = lax.rsqrt(sum_squares / feature_total + epsilon)
    cross_scaled = inv_rms * sum_cross
    return (inv_rms[:, None] * (out_grad - flat_out * (inv_rms * cross_scaled / feature_total)[:, None])).astype(jnp.bfloat16)

def backward_local(queries, key_rows, value_rows, d_out, weights, within, carried_in, state_low):
    value_grad = product('hts,thd->shd', weights, d_out)
    weight_grad = product('thd,shd->hts', d_out, value_rows)
    score_grad = (weight_grad * within).astype(jnp.bfloat16)
    query_grad = product('hts,shd->thd', score_grad, key_rows) + carried_in[:, :, None] * product('the,hde->thd', d_out, state_low)
    key_grad = product('hts,thd->shd', score_grad, queries)
    weighted_queries = (queries * carried_in[:, :, None]).astype(jnp.bfloat16)
    adjoint_local = product('thd,the->hde', weighted_queries, d_out)
    return (query_grad, key_grad, value_grad, adjoint_local)

def reference(queries, key_rows, value_rows, log_decay, doc_start, out_cotangent):
    span_count = N_CTX
    span_shape = (span_count, TOK_DEV, HEAD_TOTAL, DH)
    query_spans = queries.reshape(span_shape)
    key_spans = key_rows.reshape(span_shape)
    value_spans = value_rows.reshape(span_shape)
    decay_spans = log_decay.reshape(span_count, TOK_DEV, HEAD_TOTAL)
    start_spans = doc_start.reshape(span_count, TOK_DEV // BLK)
    cotangent_spans = out_cotangent.reshape(span_count, TOK_DEV, HEAD_TOTAL * DH)

    def span_states(span_items):
        key_span, value_span, decay_span, start_span = span_items
        carried_in, to_end, within = decay_terms(decay_span, start_span)
        weighted_keys = (key_span * to_end[:, :, None]).astype(jnp.bfloat16)
        end_state = product('shd,she->hde', weighted_keys, value_span)
        return (carried_in[-1], end_state)
    totals, end_states = lax.map(span_states, (key_spans, value_spans, decay_spans, start_spans))
    start_pair = (jnp.ones((HEAD_TOTAL,), jnp.float32), jnp.zeros((HEAD_TOTAL, DH, DH), jnp.float32))

    def forward_step(carried, element):
        return (chain_combine(carried, element), carried)
    _, prefix = lax.scan(forward_step, start_pair, (totals, end_states))
    state_in = prefix[1]

    def span_backward(span_items):
        query_span, key_span, value_span, decay_span, start_span, cotangent_span, state_span = span_items
        carried_in, to_end, within = decay_terms(decay_span, start_span)
        weights, within_out, weighted_keys, end_state = forward_local(query_span, key_span, value_span, to_end, within)
        state_low = state_span.astype(jnp.bfloat16)
        mixed_out = within_out + carried_in[:, :, None] * product('thd,hde->the', query_span, state_low)
        flat_out = mixed_out.reshape(TOK_DEV, HEAD_TOTAL * DH)
        out_grad = cotangent_span.astype(jnp.float32)
        sum_squares = lax.optimization_barrier(jnp.sum(flat_out * flat_out, axis=1))
        sum_cross = lax.optimization_barrier(jnp.sum(out_grad * flat_out, axis=1))
        d_out = norm_backward(flat_out, out_grad, sum_squares, sum_cross, HEAD_TOTAL * DH).reshape(TOK_DEV, HEAD_TOTAL, DH)
        query_grad, key_part, value_part, adjoint_local = backward_local(query_span, key_span, value_span, d_out, weights, within, carried_in, state_low)
        return (query_grad.reshape(TOK_DEV, HEAD_TOTAL * DH).astype(jnp.bfloat16), key_part, value_part, adjoint_local)
    query_grads, key_parts, value_parts, adjoint_locals = lax.map(span_backward, (query_spans, key_spans, value_spans, decay_spans, start_spans, cotangent_spans, state_in))

    def reverse_step(carried, element):
        return (chain_combine(carried, element), carried)
    _, suffix = lax.scan(reverse_step, start_pair, (totals, adjoint_locals), reverse=True)
    later_adjoint = suffix[1]

    def span_final(span_items):
        key_part, value_part, key_span, value_span, decay_span, start_span, later_span = span_items
        carried_in, to_end, within = decay_terms(decay_span, start_span)
        weighted_keys = (key_span * to_end[:, :, None]).astype(jnp.bfloat16)
        later_low = later_span.astype(jnp.bfloat16)
        key_grad = key_part + to_end[:, :, None] * product('she,hde->shd', value_span, later_low)
        value_grad = value_part + product('shd,hde->she', weighted_keys, later_low)
        return (key_grad.reshape(TOK_DEV, HEAD_TOTAL * DH).astype(jnp.bfloat16), value_grad.reshape(TOK_DEV, HEAD_TOTAL * DH).astype(jnp.bfloat16))
    key_grads, value_grads = lax.map(span_final, (key_parts, value_parts, key_spans, value_spans, decay_spans, start_spans, later_adjoint))
    return (query_grads.reshape(SEQUENCE_LENGTH, HEAD_TOTAL * DH), key_grads.reshape(SEQUENCE_LENGTH, HEAD_TOTAL * DH), value_grads.reshape(SEQUENCE_LENGTH, HEAD_TOTAL * DH))
```

```python
import functools

import jax
import jax.numpy as jnp
from jax import lax
from jax.experimental import pallas as pl
from jax.experimental.pallas import tpu as pltpu
from jax.sharding import PartitionSpec as P

epsilon = 1e-05
DIM = 128
X_SIZE = 4
BF16, F32 = jnp.bfloat16, jnp.float32
HIGHEST = lax.Precision.HIGHEST


def dot(left, right, left_dim=1, right_dim=0, precision=None):
    return lax.dot_general(
        left,
        right,
        (((left_dim,), (right_dim,)), ((), ())),
        precision=precision,
        preferred_element_type=F32,
    )


def kernel(
    nx,
    nz,
    nh,
    q_ref,
    k_ref,
    v_ref,
    decay_ref,
    doc_ref,
    g_ref,
    dq_ref,
    dk_ref,
    dv_ref,
    within_s,
    cin_s,
    end_s,
    weights_s,
    wk_s,
    d_s,
    mixed_s,
    kg_s,
    low_s,
    dec_own,
    dec_x,
    dec_tot,
    dec_z,
    local_s,
    xin_s,
    tot_s,
    zin_s,
    zout_s,
    zback_s,
    xout_s,
    state_s,
    stat_own,
    stat_in,
    x_send,
    x_recv,
    z_send,
    z_recv,
    h_send,
    h_recv,
):
    rows = q_ref.shape[0]
    heads = q_ref.shape[1] // DIM
    quarter = heads // nx
    qrows = quarter * DIM
    chunk = qrows // nz
    feature_total = heads * DIM * nh
    ctx, me_h = lax.axis_index("ctx"), lax.axis_index("head")
    me_z, me_x = ctx // nx, ctx % nx
    waits = []

    def x_peer(o):
        return lax.rem(me_x + o, nx)

    def z_peer(o):
        return lax.rem(me_z + o, nz)

    def h_peer(o):
        return lax.rem(me_h + o, nh)

    def x_id(o):
        return {"ctx": me_z * nx + x_peer(o)}

    def z_id(o):
        return {"ctx": z_peer(o) * nx + me_x}

    def h_id(o):
        return {"head": h_peer(o)}

    def exchange(count, source, target, send, recv, device):
        copies = []
        for o in range(1, count):
            copy = pltpu.make_async_remote_copy(
                src_ref=source(o),
                dst_ref=target,
                send_sem=send.at[o],
                recv_sem=recv.at[o],
                device_id=device(o),
                device_id_type=pl.DeviceIdType.MESH,
            )
            copy.start()
            copies.append(copy)
        waits.extend(copies)
        return copies

    def arrive(copies):
        for copy in copies:
            copy.wait_recv()

    def lanes(h):
        return pl.ds(pl.multiple_of(h * DIM, DIM), DIM)

    def per_head(body, start=0):
        return lax.fori_loop(0, heads, body, start, unroll=2)

    barrier = pltpu.get_barrier_semaphore()
    peers = [x_id(o) for o in range(1, nx)]
    peers += [z_id(o) for o in range(1, nz)]
    peers += [h_id(o) for o in range(1, nh)]
    for peer in peers:
        pl.semaphore_signal(barrier, inc=1, device_id=peer, device_id_type=pl.DeviceIdType.MESH)

    down = lax.broadcasted_iota(jnp.int32, (rows, rows), 0)
    across = lax.broadcasted_iota(jnp.int32, (rows, rows), 1)
    eye = down == across
    lower = down >= across
    blocks = doc_ref.shape[0]
    size = rows // blocks
    reset_down = jnp.zeros((rows, rows), F32)
    reset_across = jnp.zeros((rows, rows), F32)
    for b in range(blocks):
        at = jnp.where(doc_ref[b] < size, b * size + doc_ref[b], -1)
        reset_down = reset_down + jnp.where(down == at, 1.0, 0.0)
        reset_across = reset_across + jnp.where(across == at, 1.0, 0.0)
    ones_lower = jnp.where(lower, 1.0, 0.0)
    segment = dot(ones_lower, reset_down)
    segment_across = dot(reset_across, jnp.where(down <= across, 1.0, 0.0))
    causal = lower & (segment == segment_across)
    cumulative = dot(ones_lower, decay_ref[...], precision=HIGHEST)
    first = segment == 0.0
    to_last = segment == segment[rows - 1 : rows, :]
    for h in range(heads):
        gone = jnp.broadcast_to(cumulative[:, h : h + 1], (rows, DIM))
        gone_across = jnp.sum(jnp.where(eye, gone, 0.0), axis=0, keepdims=True)
        gap = jnp.where(causal, gone - gone_across, 0.0)
        within_s[h] = jnp.where(causal, jnp.exp(gap), 0.0)
        carried = jnp.where(first, jnp.exp(gone), 0.0)
        cin_s[h] = carried
        end_s[h] = jnp.where(to_last, jnp.exp(gone[rows - 1 : rows, :] - gone), 0.0)
        dec_own[h : h + 1, :] = carried[rows - 1 : rows, :]

    def end_state(h, carry):
        wk = (k_ref[:, lanes(h)].astype(F32) * end_s[h]).astype(BF16)
        wk_s[h] = wk
        local_s[0, lanes(h), :] = dot(wk, v_ref[:, lanes(h)], 0, 0)
        return carry

    per_head(end_state)

    pl.semaphore_wait(barrier, len(peers))
    dec_copies = exchange(nx, lambda o: dec_own, dec_x.at[me_x], x_send.at[0], x_recv.at[0], x_id)

    def chain_x_in(c):
        own = pl.ds(pl.multiple_of(me_x * qrows, qrows), qrows)
        copies = exchange(
            nx,
            lambda o: local_s.at[c, pl.ds(pl.multiple_of(x_peer(o) * qrows, qrows), qrows)],
            xin_s.at[c, me_x],
            x_send.at[1 + 2 * c],
            x_recv.at[1 + 2 * c],
            x_id,
        )
        xin_s[c, me_x] = local_s[c, own, :]
        return copies

    def decay_x(place, i):
        return dec_x[place, pl.ds(me_x * quarter + i, 1), :]

    def chain_z_in(c, x_copies):
        arrive(x_copies)
        for i in range(quarter):
            part = pl.ds(i * DIM, DIM)
            order = range(nx) if c == 0 else range(nx - 1, -1, -1)
            total = None
            for place in order:
                term = xin_s[c, place, part, :]
                total = term if total is None else decay_x(place, i) * total + term
            tot_s[c, part, :] = total
        copies = exchange(
            nz,
            lambda o: tot_s.at[c, pl.ds(pl.multiple_of(z_peer(o) * chunk, chunk), chunk)],
            zin_s.at[c, me_z],
            z_send.at[1 + 2 * c],
            z_recv.at[1 + 2 * c],
            z_id,
        )
        zin_s[c, me_z] = tot_s[c, pl.ds(pl.multiple_of(me_z * chunk, chunk), chunk), :]
        return copies

    def chain_out(c, z_copies):
        arrive(z_copies)
        head = me_x * quarter + (me_z * chunk) // DIM
        state = jnp.zeros((chunk, DIM), F32)
        for place in range(nz) if c == 0 else range(nz - 1, -1, -1):
            zout_s[c, place] = state
            state = dec_z[place, pl.ds(head, 1), :] * state + zin_s[c, place]
        mine = pl.ds(pl.multiple_of(me_z * chunk, chunk), chunk)
        copies = exchange(
            nz,
            lambda o: zout_s.at[c, z_peer(o)],
            zback_s.at[c, mine],
            z_send.at[2 + 2 * c],
            z_recv.at[2 + 2 * c],
            z_id,
        )
        zback_s[c, mine, :] = zout_s[c, me_z]
        arrive(copies)
        for i in range(quarter):
            part = pl.ds(i * DIM, DIM)
            state = zback_s[c, part, :]
            for place in range(nx) if c == 0 else range(nx - 1, -1, -1):
                xout_s[c, place, part, :] = state
                state = decay_x(place, i) * state + xin_s[c, place, part, :]
        own = pl.ds(pl.multiple_of(me_x * qrows, qrows), qrows)
        copies = exchange(
            nx,
            lambda o: xout_s.at[c, x_peer(o)],
            state_s.at[c, own],
            x_send.at[2 + 2 * c],
            x_recv.at[2 + 2 * c],
            x_id,
        )
        state_s[c, own, :] = xout_s[c, me_x]
        arrive(copies)

    x_copies = chain_x_in(0)
    dec_x[me_x] = dec_own[...]
    arrive(dec_copies)
    total_decay = dec_x[0]
    for place in range(1, nx):
        total_decay = total_decay * dec_x[place]
    dec_tot[...] = total_decay
    dec_copies = exchange(nz, lambda o: dec_tot, dec_z.at[me_z], z_send.at[0], z_recv.at[0], z_id)
    dec_z[me_z] = total_decay

    z_copies = chain_z_in(0, x_copies)

    def within_out(h, carry):
        scores = dot(q_ref[:, lanes(h)], k_ref[:, lanes(h)], 1, 1)
        weights = (scores * within_s[h]).astype(BF16)
        weights_s[h] = weights
        mixed_s[h] = dot(weights, v_ref[:, lanes(h)])
        return carry

    per_head(within_out)
    arrive(dec_copies)
    chain_out(0, z_copies)

    def mix(h, sums):
        low = state_s[0, lanes(h), :].astype(BF16)
        low_s[h] = low
        mixed = mixed_s[h] + cin_s[h] * dot(q_ref[:, lanes(h)], low)
        mixed_s[h] = mixed
        return sums[0] + mixed * mixed, sums[1] + g_ref[:, lanes(h)].astype(F32) * mixed

    zero = jnp.zeros((rows, DIM), F32)
    sums = per_head(mix, (zero, zero))

    def as_row(total):
        column = jnp.broadcast_to(jnp.sum(total, axis=1, keepdims=True), (rows, rows))
        return jnp.sum(jnp.where(eye, column, 0.0), axis=0, keepdims=True)

    def as_column(row):
        spread = jnp.where(eye, jnp.broadcast_to(row, (rows, rows)), 0.0)
        return jnp.broadcast_to(jnp.sum(spread, axis=1, keepdims=True), (rows, DIM))

    stat_own[...] = jnp.zeros_like(stat_own)
    stat_own[0:1, :] = as_row(sums[0])
    stat_own[1:2, :] = as_row(sums[1])
    copies = exchange(nh, lambda o: stat_own, stat_in.at[me_h], h_send, h_recv, h_id)
    stat_in[me_h] = stat_own[...]
    arrive(copies)
    totals = stat_in[0]
    for place in range(1, nh):
        totals = totals + stat_in[place]
    inv_row = lax.rsqrt(totals[0:1, :] / feature_total + epsilon)
    inv = as_column(inv_row)
    pull = as_column(inv_row * (inv_row * totals[1:2, :]) / feature_total)

    def adjoint(h, carry):
        grad = g_ref[:, lanes(h)].astype(F32)
        d_out = (inv * (grad - mixed_s[h] * pull)).astype(BF16)
        d_s[h] = d_out
        wq = (q_ref[:, lanes(h)].astype(F32) * cin_s[h]).astype(BF16)
        local_s[1, lanes(h), :] = dot(wq, d_out, 0, 0)
        return carry

    per_head(adjoint)
    x_copies = chain_x_in(1)

    def scores_back(h, carry):
        d_out = d_s[h]
        mixed_s[h] = dot(weights_s[h], d_out, 0, 0)
        score_grad = (dot(d_out, v_ref[:, lanes(h)], 1, 1) * within_s[h]).astype(BF16)
        weights_s[h] = score_grad
        kg_s[h] = dot(score_grad, q_ref[:, lanes(h)], 0, 0)
        return carry

    def query_back(h, carry):
        carried = cin_s[h] * dot(d_s[h], low_s[h], 1, 1)
        grad = dot(weights_s[h], k_ref[:, lanes(h)]) + carried
        dq_ref[:, lanes(h)] = grad.astype(BF16)
        return carry

    z_copies = chain_z_in(1, x_copies)
    per_head(scores_back)
    per_head(query_back)
    chain_out(1, z_copies)

    def finish(h, carry):
        later = state_s[1, lanes(h), :].astype(BF16)
        key_grad = kg_s[h] + end_s[h] * dot(v_ref[:, lanes(h)], later, 1, 1)
        dk_ref[:, lanes(h)] = key_grad.astype(BF16)
        value_grad = mixed_s[h] + dot(wk_s[h], later)
        dv_ref[:, lanes(h)] = value_grad.astype(BF16)
        return carry

    per_head(finish)
    for copy in waits:
        copy.wait_send()


def local(nx, nz, nh, queries, key_rows, value_rows, log_decay, doc_start, out_cotangent):
    rows, width = queries.shape
    heads = width // DIM
    quarter = heads // nx * DIM
    chunk = quarter // nz
    vmem = pl.BlockSpec(memory_space=pltpu.VMEM)
    smem = pl.BlockSpec(memory_space=pltpu.SMEM)
    square = pltpu.VMEM((heads, rows, DIM), F32)
    square_low = pltpu.VMEM((heads, rows, DIM), BF16)
    out = jax.ShapeDtypeStruct((rows, width), BF16)
    return pl.pallas_call(
        functools.partial(kernel, nx, nz, nh),
        out_shape=(out, out, out),
        in_specs=[vmem, vmem, vmem, vmem, smem, vmem],
        out_specs=(vmem, vmem, vmem),
        scratch_shapes=[
            square,
            square,
            square,
            square_low,
            square_low,
            square_low,
            square,
            square,
            pltpu.VMEM((heads, DIM, DIM), BF16),
            pltpu.VMEM((heads, DIM), F32),
            pltpu.VMEM((nx, heads, DIM), F32),
            pltpu.VMEM((heads, DIM), F32),
            pltpu.VMEM((nz, heads, DIM), F32),
            pltpu.VMEM((2, heads * DIM, DIM), F32),
            pltpu.VMEM((2, nx, quarter, DIM), F32),
            pltpu.VMEM((2, quarter, DIM), F32),
            pltpu.VMEM((2, nz, chunk, DIM), F32),
            pltpu.VMEM((2, nz, chunk, DIM), F32),
            pltpu.VMEM((2, quarter, DIM), F32),
            pltpu.VMEM((2, nx, quarter, DIM), F32),
            pltpu.VMEM((2, heads * DIM, DIM), F32),
            pltpu.VMEM((8, DIM), F32),
            pltpu.VMEM((nh, 8, DIM), F32),
            pltpu.SemaphoreType.DMA((5, nx)),
            pltpu.SemaphoreType.DMA((5, nx)),
            pltpu.SemaphoreType.DMA((5, nz)),
            pltpu.SemaphoreType.DMA((5, nz)),
            pltpu.SemaphoreType.DMA((nh,)),
            pltpu.SemaphoreType.DMA((nh,)),
        ],
        compiler_params=pltpu.CompilerParams(collective_id=0, has_side_effects=True),
    )(queries, key_rows, value_rows, log_decay, doc_start, out_cotangent)


def solution(mesh):
    nx = X_SIZE
    nz, nh = mesh.shape["ctx"] // nx, mesh.shape["head"]
    wide = P("ctx", "head")
    return jax.shard_map(
        functools.partial(local, nx, nz, nh),
        mesh=mesh,
        in_specs=(wide, wide, wide, wide, P("ctx"), wide),
        out_specs=(wide, wide, wide),
        check_vma=False,
    )
```

```python
import functools

import jax
import jax.numpy as jnp
from jax import lax
from jax.experimental import pallas as pl
from jax.experimental.pallas import tpu as pltpu
from jax.sharding import PartitionSpec as P

epsilon = 1e-05
DIM = 128
X_SIZE = 4
BF16, F32 = jnp.bfloat16, jnp.float32
HIGHEST = lax.Precision.HIGHEST


def dot(left, right, left_dim=1, right_dim=0, precision=None):
    return lax.dot_general(
        left,
        right,
        (((left_dim,), (right_dim,)), ((), ())),
        precision=precision,
        preferred_element_type=F32,
    )


def kernel(
    nx,
    nz,
    nh,
    q_ref,
    k_ref,
    v_ref,
    decay_ref,
    doc_ref,
    g_ref,
    dq_ref,
    dk_ref,
    dv_ref,
    within_s,
    cin_s,
    end_s,
    weights_s,
    wk_s,
    d_s,
    mixed_s,
    kg_s,
    low_s,
    dec_own,
    dec_x,
    dec_tot,
    dec_z,
    local_s,
    xin_s,
    tot_s,
    zin_s,
    zout_s,
    zback_s,
    xout_s,
    state_s,
    stat_own,
    stat_in,
    x_send,
    x_recv,
    z_send,
    z_recv,
    h_send,
    h_recv,
):
    rows = q_ref.shape[0]
    heads = q_ref.shape[1] // DIM
    quarter = heads // nx
    qrows = quarter * DIM
    chunk = DIM // nz
    feature_total = heads * DIM * nh
    ctx, me_h = lax.axis_index("ctx"), lax.axis_index("head")
    me_z, me_x = ctx // nx, ctx % nx
    waits = []

    def x_peer(o):
        return lax.rem(me_x + o, nx)

    def z_peer(o):
        return lax.rem(me_z + o, nz)

    def h_peer(o):
        return lax.rem(me_h + o, nh)

    def x_id(o):
        return {"ctx": me_z * nx + x_peer(o)}

    def z_id(o):
        return {"ctx": z_peer(o) * nx + me_x}

    def h_id(o):
        return {"head": h_peer(o)}

    def exchange(count, source, target, send, recv, device):
        copies = []
        for o in range(1, count):
            copy = pltpu.make_async_remote_copy(
                src_ref=source(o),
                dst_ref=target,
                send_sem=send.at[o],
                recv_sem=recv.at[o],
                device_id=device(o),
                device_id_type=pl.DeviceIdType.MESH,
            )
            copy.start()
            copies.append(copy)
        waits.extend(copies)
        return copies

    def arrive(copies):
        for copy in copies:
            copy.wait_recv()

    def lanes(h):
        return pl.ds(h * DIM, DIM)

    barrier = pltpu.get_barrier_semaphore()
    peers = [x_id(o) for o in range(1, nx)]
    peers += [z_id(o) for o in range(1, nz)]
    peers += [h_id(o) for o in range(1, nh)]
    for peer in peers:
        pl.semaphore_signal(barrier, inc=1, device_id=peer, device_id_type=pl.DeviceIdType.MESH)

    down = lax.broadcasted_iota(jnp.int32, (rows, rows), 0)
    across = lax.broadcasted_iota(jnp.int32, (rows, rows), 1)
    eye = down == across
    lower = down >= across
    blocks = doc_ref.shape[0]
    size = rows // blocks
    reset_down = jnp.zeros((rows, rows), F32)
    reset_across = jnp.zeros((rows, rows), F32)
    for b in range(blocks):
        at = jnp.where(doc_ref[b] < size, b * size + doc_ref[b], -1)
        reset_down = reset_down + jnp.where(down == at, 1.0, 0.0)
        reset_across = reset_across + jnp.where(across == at, 1.0, 0.0)
    ones_lower = jnp.where(lower, 1.0, 0.0)
    ones_upper = jnp.where(down <= across, 1.0, 0.0)
    segment = dot(ones_lower, reset_down)
    segment_across = dot(reset_across, ones_upper)
    causal = lower & (segment == segment_across)
    decays = decay_ref[...]
    cumulative = dot(ones_lower, decays, 1, 1, precision=HIGHEST)
    cumulative_across = dot(decays, ones_upper, precision=HIGHEST)
    first = segment == 0.0
    to_last = segment == segment[rows - 1 : rows, :]
    span_end = jnp.broadcast_to(cumulative_across[:, rows - 1 : rows], (heads, DIM))
    dec_own[...] = jnp.where(first[rows - 1 : rows, :], jnp.exp(span_end), 0.0)
    dec_x[me_x] = dec_own[...]

    def prepare(h):
        gone = jnp.broadcast_to(cumulative[:, h : h + 1], (rows, DIM))
        cin_s[h] = jnp.where(first, jnp.exp(gone), 0.0)
        to_end = jnp.where(to_last, jnp.exp(gone[rows - 1 : rows, :] - gone), 0.0)
        end_s[h] = to_end
        wk = (k_ref[:, lanes(h)].astype(F32) * to_end).astype(BF16)
        wk_s[h] = wk
        local_s[0, lanes(h), :] = dot(wk, v_ref[:, lanes(h)], 0, 0)

    def piece_heads(i):
        return [j * quarter + i for j in range(nx)]

    def x_at(c, back, i):
        return 1 + (c * 2 + back) * quarter + i

    def local_part(place, i):
        return pl.ds(pl.multiple_of(place * qrows + i * DIM, DIM), DIM)

    def chunk_part(place, i):
        return pl.ds(pl.multiple_of(i * DIM + place * chunk, chunk), chunk)

    def x_order(c):
        return range(nx) if c == 0 else range(nx - 1, -1, -1)

    def decay_x(place, i):
        return dec_x[place, pl.ds(me_x * quarter + i, 1), :]

    def send_local(c, i):
        at = x_at(c, 0, i)
        copies = exchange(
            nx,
            lambda o: local_s.at[c, local_part(x_peer(o), i)],
            xin_s.at[c, me_x, pl.ds(i * DIM, DIM)],
            x_send.at[at],
            x_recv.at[at],
            x_id,
        )
        xin_s[c, me_x, pl.ds(i * DIM, DIM), :] = local_s[c, local_part(me_x, i), :]
        return copies

    def send_total(c, i, copies):
        arrive(copies)
        part = pl.ds(i * DIM, DIM)
        total = None
        for place in x_order(c):
            term = xin_s[c, place, part, :]
            total = term if total is None else decay_x(place, i) * total + term
        tot_s[c, part, :] = total
        at = x_at(c, 0, i)
        copies = exchange(
            nz,
            lambda o: tot_s.at[c, chunk_part(z_peer(o), i)],
            zin_s.at[c, i, me_z],
            z_send.at[at],
            z_recv.at[at],
            z_id,
        )
        zin_s[c, i, me_z] = tot_s[c, chunk_part(me_z, i), :]
        return copies

    def send_scanned(c, i, copies):
        arrive(copies)
        state = jnp.zeros((chunk, DIM), F32)
        for place in range(nz) if c == 0 else range(nz - 1, -1, -1):
            zout_s[c, i, place] = state
            decay = dec_z[place, pl.ds(me_x * quarter + i, 1), :]
            state = decay * state + zin_s[c, i, place]
        at = x_at(c, 1, i)
        copies = exchange(
            nz,
            lambda o: zout_s.at[c, i, z_peer(o)],
            zback_s.at[c, chunk_part(me_z, i)],
            z_send.at[at],
            z_recv.at[at],
            z_id,
        )
        zback_s[c, chunk_part(me_z, i), :] = zout_s[c, i, me_z]
        return copies

    def send_states(c, i, copies):
        arrive(copies)
        part = pl.ds(i * DIM, DIM)
        state = zback_s[c, part, :]
        for place in x_order(c):
            xout_s[c, place, part, :] = state
            state = decay_x(place, i) * state + xin_s[c, place, part, :]
        at = x_at(c, 1, i)
        copies = exchange(
            nx,
            lambda o: xout_s.at[c, x_peer(o), part],
            state_s.at[c, local_part(me_x, i)],
            x_send.at[at],
            x_recv.at[at],
            x_id,
        )
        state_s[c, local_part(me_x, i), :] = xout_s[c, me_x, part, :]
        return copies

    pieces = range(quarter)
    x_copies, dec_copies = [], None
    for i in pieces:
        for h in piece_heads(i):
            prepare(h)
        if i == 0:
            pl.semaphore_wait(barrier, len(peers))
            dec_copies = exchange(
                nx, lambda o: dec_own, dec_x.at[me_x], x_send.at[0], x_recv.at[0], x_id
            )
        x_copies.append(send_local(0, i))

    arrive(dec_copies)
    total_decay = dec_x[0]
    for place in range(1, nx):
        total_decay = total_decay * dec_x[place]
    dec_tot[...] = total_decay
    dec_copies = exchange(nz, lambda o: dec_tot, dec_z.at[me_z], z_send.at[0], z_recv.at[0], z_id)
    dec_z[me_z] = total_decay
    z_copies = [send_total(0, i, x_copies[i]) for i in pieces]

    for h in range(heads):
        gone = jnp.broadcast_to(cumulative[:, h : h + 1], (rows, DIM))
        gap = jnp.where(causal, gone - cumulative_across[h : h + 1, :], 0.0)
        within = jnp.where(causal, jnp.exp(gap), 0.0)
        within_s[h] = within
        scores = dot(q_ref[:, lanes(h)], k_ref[:, lanes(h)], 1, 1)
        weights = (scores * within).astype(BF16)
        weights_s[h] = weights
        mixed_s[h] = dot(weights, v_ref[:, lanes(h)])

    arrive(dec_copies)
    z_copies = [send_scanned(0, i, z_copies[i]) for i in pieces]
    x_copies = [send_states(0, i, z_copies[i]) for i in pieces]
    squares = jnp.zeros((rows, DIM), F32)
    crosses = jnp.zeros((rows, DIM), F32)
    for i in pieces:
        arrive(x_copies[i])
        for h in piece_heads(i):
            low = state_s[0, lanes(h), :].astype(BF16)
            low_s[h] = low
            mixed = mixed_s[h] + cin_s[h] * dot(q_ref[:, lanes(h)], low)
            mixed_s[h] = mixed
            squares = squares + mixed * mixed
            crosses = crosses + g_ref[:, lanes(h)].astype(F32) * mixed

    def as_row(total):
        column = jnp.broadcast_to(jnp.sum(total, axis=1, keepdims=True), (rows, rows))
        return jnp.sum(jnp.where(eye, column, 0.0), axis=0, keepdims=True)

    def as_column(row):
        spread = jnp.where(eye, jnp.broadcast_to(row, (rows, rows)), 0.0)
        return jnp.broadcast_to(jnp.sum(spread, axis=1, keepdims=True), (rows, DIM))

    stat_own[...] = jnp.zeros_like(stat_own)
    stat_own[0:1, :] = as_row(squares)
    stat_own[1:2, :] = as_row(crosses)
    copies = exchange(nh, lambda o: stat_own, stat_in.at[me_h], h_send, h_recv, h_id)
    stat_in[me_h] = stat_own[...]
    arrive(copies)
    totals = stat_in[0]
    for place in range(1, nh):
        totals = totals + stat_in[place]
    inv_row = lax.rsqrt(totals[0:1, :] / feature_total + epsilon)
    inv = as_column(inv_row)
    pull = as_column(inv_row * (inv_row * totals[1:2, :]) / feature_total)

    x_copies = []
    for i in pieces:
        for h in piece_heads(i):
            grad = g_ref[:, lanes(h)].astype(F32)
            d_out = (inv * (grad - mixed_s[h] * pull)).astype(BF16)
            d_s[h] = d_out
            wq = (q_ref[:, lanes(h)].astype(F32) * cin_s[h]).astype(BF16)
            local_s[1, lanes(h), :] = dot(wq, d_out, 0, 0)
        x_copies.append(send_local(1, i))

    def scores_back(h):
        d_out = d_s[h]
        mixed_s[h] = dot(weights_s[h], d_out, 0, 0)
        score_grad = (dot(d_out, v_ref[:, lanes(h)], 1, 1) * within_s[h]).astype(BF16)
        kg_s[h] = dot(score_grad, q_ref[:, lanes(h)], 0, 0)
        carried = cin_s[h] * dot(d_out, low_s[h], 1, 1)
        dq_ref[:, lanes(h)] = (dot(score_grad, k_ref[:, lanes(h)]) + carried).astype(BF16)

    z_copies = [send_total(1, i, x_copies[i]) for i in pieces]
    for h in range(heads):
        scores_back(h)
    z_copies = [send_scanned(1, i, z_copies[i]) for i in pieces]
    x_copies = [send_states(1, i, z_copies[i]) for i in pieces]
    for i in pieces:
        arrive(x_copies[i])
        for h in piece_heads(i):
            later = state_s[1, lanes(h), :].astype(BF16)
            key_grad = kg_s[h] + end_s[h] * dot(v_ref[:, lanes(h)], later, 1, 1)
            dk_ref[:, lanes(h)] = key_grad.astype(BF16)
            value_grad = mixed_s[h] + dot(wk_s[h], later)
            dv_ref[:, lanes(h)] = value_grad.astype(BF16)
    for copy in waits:
        copy.wait_send()


def hand_on(a_ref, b_ref, c_ref, a_out, b_out, c_out, held, in_sem, out_sem):
    reads = [
        pltpu.make_async_copy(ref, held.at[n], in_sem.at[n])
        for n, ref in enumerate((a_ref, b_ref, c_ref))
    ]
    writes = [
        pltpu.make_async_copy(held.at[n], ref, out_sem.at[n])
        for n, ref in enumerate((a_out, b_out, c_out))
    ]
    for read in reads:
        read.start()
    for read, write in zip(reads, writes):
        read.wait()
        write.start()
    for write in writes:
        write.wait()


def local(nx, nz, nh, queries, key_rows, value_rows, log_decay, doc_start, out_cotangent):
    rows, width = queries.shape
    heads = width // DIM
    quarter = heads // nx * DIM
    chunk = DIM // nz
    pieces = quarter // DIM
    slots = 1 + 4 * pieces
    vmem = pl.BlockSpec(memory_space=pltpu.VMEM)
    smem = pl.BlockSpec(memory_space=pltpu.SMEM)
    square = pltpu.VMEM((heads, rows, DIM), F32)
    square_low = pltpu.VMEM((heads, rows, DIM), BF16)
    out = jax.ShapeDtypeStruct((rows, width), BF16)
    grads = pl.pallas_call(
        functools.partial(kernel, nx, nz, nh),
        out_shape=(out, out, out),
        in_specs=[vmem, vmem, vmem, vmem, smem, vmem],
        out_specs=(vmem, vmem, vmem),
        scratch_shapes=[
            square,
            square,
            square,
            square_low,
            square_low,
            square_low,
            square,
            square,
            pltpu.VMEM((heads, DIM, DIM), BF16),
            pltpu.VMEM((heads, DIM), F32),
            pltpu.VMEM((nx, heads, DIM), F32),
            pltpu.VMEM((heads, DIM), F32),
            pltpu.VMEM((nz, heads, DIM), F32),
            pltpu.VMEM((2, heads * DIM, DIM), F32),
            pltpu.VMEM((2, nx, quarter, DIM), F32),
            pltpu.VMEM((2, quarter, DIM), F32),
            pltpu.VMEM((2, pieces, nz, chunk, DIM), F32),
            pltpu.VMEM((2, pieces, nz, chunk, DIM), F32),
            pltpu.VMEM((2, quarter, DIM), F32),
            pltpu.VMEM((2, nx, quarter, DIM), F32),
            pltpu.VMEM((2, heads * DIM, DIM), F32),
            pltpu.VMEM((8, DIM), F32),
            pltpu.VMEM((nh, 8, DIM), F32),
            pltpu.SemaphoreType.DMA((slots, nx)),
            pltpu.SemaphoreType.DMA((slots, nx)),
            pltpu.SemaphoreType.DMA((slots, nz)),
            pltpu.SemaphoreType.DMA((slots, nz)),
            pltpu.SemaphoreType.DMA((nh,)),
            pltpu.SemaphoreType.DMA((nh,)),
        ],
        compiler_params=pltpu.CompilerParams(collective_id=0, has_side_effects=True),
    )(queries, key_rows, value_rows, log_decay.T, doc_start, out_cotangent)
    anywhere = pl.BlockSpec(memory_space=pl.ANY)
    return pl.pallas_call(
        hand_on,
        out_shape=(out, out, out),
        in_specs=[anywhere] * 3,
        out_specs=(anywhere,) * 3,
        scratch_shapes=[
            pltpu.VMEM((3, rows, width), BF16),
            pltpu.SemaphoreType.DMA((3,)),
            pltpu.SemaphoreType.DMA((3,)),
        ],
    )(*grads)


def solution(mesh):
    nx = X_SIZE
    nz, nh = mesh.shape["ctx"] // nx, mesh.shape["head"]
    wide = P("ctx", "head")
    return jax.shard_map(
        functools.partial(local, nx, nz, nh),
        mesh=mesh,
        in_specs=(wide, wide, wide, wide, P("ctx"), wide),
        out_specs=(wide, wide, wide),
        check_vma=False,
    )
```

```python
import functools

import jax
import jax.numpy as jnp
from jax import lax
from jax.experimental import pallas as pl
from jax.experimental.pallas import tpu as pltpu
from jax.sharding import PartitionSpec as P

epsilon = 1e-05
DIM = 128
X_SIZE = 4
BF16, F32 = jnp.bfloat16, jnp.float32
HIGHEST = lax.Precision.HIGHEST


def dot(left, right, left_dim=1, right_dim=0, precision=None):
    return lax.dot_general(
        left,
        right,
        (((left_dim,), (right_dim,)), ((), ())),
        precision=precision,
        preferred_element_type=F32,
    )


def kernel(
    nx,
    nz,
    nh,
    q_ref,
    k_ref,
    v_ref,
    decay_ref,
    doc_ref,
    g_ref,
    dq_ref,
    dk_ref,
    dv_ref,
    within_s,
    cin_s,
    end_s,
    weights_s,
    wk_s,
    d_s,
    mixed_s,
    kg_s,
    low_s,
    dec_own,
    dec_x,
    dec_tot,
    dec_z,
    local_s,
    xin_s,
    tot_s,
    zin_s,
    zout_s,
    zback_s,
    xout_s,
    state_s,
    stat_own,
    stat_in,
    x_send,
    x_recv,
    z_send,
    z_recv,
    h_send,
    h_recv,
):
    rows = q_ref.shape[0]
    heads = q_ref.shape[1] // DIM
    quarter = heads // nx
    qrows = quarter * DIM
    chunk = DIM // nz
    feature_total = heads * DIM * nh
    ctx, me_h = lax.axis_index("ctx"), lax.axis_index("head")
    me_z, me_x = ctx // nx, ctx % nx
    waits = []

    def x_peer(o):
        return lax.rem(me_x + o, nx)

    def z_peer(o):
        return lax.rem(me_z + o, nz)

    def h_peer(o):
        return lax.rem(me_h + o, nh)

    def x_id(o):
        return {"ctx": me_z * nx + x_peer(o)}

    def z_id(o):
        return {"ctx": z_peer(o) * nx + me_x}

    def h_id(o):
        return {"head": h_peer(o)}

    def exchange(count, source, target, send, recv, device):
        copies = []
        for o in sorted(range(1, count), key=lambda o: -min(o, count - o)):
            copy = pltpu.make_async_remote_copy(
                src_ref=source(o),
                dst_ref=target,
                send_sem=send.at[o],
                recv_sem=recv.at[o],
                device_id=device(o),
                device_id_type=pl.DeviceIdType.MESH,
            )
            copy.start()
            copies.append(copy)
        waits.extend(copies)
        return copies

    def arrive(copies):
        for copy in copies:
            copy.wait_recv()

    def lanes(h):
        return pl.ds(h * DIM, DIM)

    barrier = pltpu.get_barrier_semaphore()
    peers = [z_id(o) for o in sorted(range(1, nz), key=lambda o: -min(o, nz - o))]
    peers += [x_id(o) for o in range(1, nx)]
    peers += [h_id(o) for o in range(1, nh)]
    for peer in peers:
        pl.semaphore_signal(barrier, inc=1, device_id=peer, device_id_type=pl.DeviceIdType.MESH)

    down = lax.broadcasted_iota(jnp.int32, (rows, rows), 0)
    across = lax.broadcasted_iota(jnp.int32, (rows, rows), 1)
    eye = down == across
    lower = down >= across
    blocks = doc_ref.shape[0]
    size = rows // blocks
    reset_down = jnp.zeros((rows, rows), F32)
    reset_across = jnp.zeros((rows, rows), F32)
    for b in range(blocks):
        at = jnp.where(doc_ref[b] < size, b * size + doc_ref[b], -1)
        reset_down = reset_down + jnp.where(down == at, 1.0, 0.0)
        reset_across = reset_across + jnp.where(across == at, 1.0, 0.0)
    ones_lower = jnp.where(lower, 1.0, 0.0)
    ones_upper = jnp.where(down <= across, 1.0, 0.0)
    segment = dot(ones_lower, reset_down)
    segment_across = dot(reset_across, ones_upper)
    causal = lower & (segment == segment_across)
    decays = decay_ref[...]
    cumulative = dot(ones_lower, decays, 1, 1, precision=HIGHEST)
    cumulative_across = dot(decays, ones_upper, precision=HIGHEST)
    first = segment == 0.0
    to_last = segment == segment[rows - 1 : rows, :]
    span_end = jnp.broadcast_to(cumulative_across[:, rows - 1 : rows], (heads, DIM))
    dec_own[...] = jnp.where(first[rows - 1 : rows, :], jnp.exp(span_end), 0.0)
    dec_x[me_x] = dec_own[...]

    def prepare(h):
        gone = jnp.broadcast_to(cumulative[:, h : h + 1], (rows, DIM))
        cin_s[h] = jnp.where(first, jnp.exp(gone), 0.0)
        to_end = jnp.where(to_last, jnp.exp(gone[rows - 1 : rows, :] - gone), 0.0)
        end_s[h] = to_end
        wk = (k_ref[:, lanes(h)].astype(F32) * to_end).astype(BF16)
        wk_s[h] = wk
        local_s[0, lanes(h), :] = dot(wk, v_ref[:, lanes(h)], 0, 0)

    def piece_heads(i):
        return [j * quarter + i for j in range(nx)]

    def x_at(c, back, i):
        return 1 + (c * 2 + back) * quarter + i

    def local_part(place, i):
        return pl.ds(pl.multiple_of(place * qrows + i * DIM, DIM), DIM)

    def chunk_part(place, i):
        return pl.ds(pl.multiple_of(i * DIM + place * chunk, chunk), chunk)

    def x_order(c):
        return range(nx) if c == 0 else range(nx - 1, -1, -1)

    def decay_x(place, i):
        return dec_x[place, pl.ds(me_x * quarter + i, 1), :]

    def send_local(c, i):
        at = x_at(c, 0, i)
        copies = exchange(
            nx,
            lambda o: local_s.at[c, local_part(x_peer(o), i)],
            xin_s.at[c, me_x, pl.ds(i * DIM, DIM)],
            x_send.at[at],
            x_recv.at[at],
            x_id,
        )
        xin_s[c, me_x, pl.ds(i * DIM, DIM), :] = local_s[c, local_part(me_x, i), :]
        return copies

    def send_total(c, i, copies):
        arrive(copies)
        part = pl.ds(i * DIM, DIM)
        total = None
        for place in x_order(c):
            term = xin_s[c, place, part, :]
            total = term if total is None else decay_x(place, i) * total + term
        tot_s[c, part, :] = total
        at = x_at(c, 0, i)
        copies = exchange(
            nz,
            lambda o: tot_s.at[c, chunk_part(z_peer(o), i)],
            zin_s.at[c, i, me_z],
            z_send.at[at],
            z_recv.at[at],
            z_id,
        )
        zin_s[c, i, me_z] = tot_s[c, chunk_part(me_z, i), :]
        return copies

    def send_scanned(c, i, copies):
        arrive(copies)
        state = jnp.zeros((chunk, DIM), F32)
        for place in range(nz) if c == 0 else range(nz - 1, -1, -1):
            zout_s[c, i, place] = state
            decay = dec_z[place, pl.ds(me_x * quarter + i, 1), :]
            state = decay * state + zin_s[c, i, place]
        at = x_at(c, 1, i)
        copies = exchange(
            nz,
            lambda o: zout_s.at[c, i, z_peer(o)],
            zback_s.at[c, chunk_part(me_z, i)],
            z_send.at[at],
            z_recv.at[at],
            z_id,
        )
        zback_s[c, chunk_part(me_z, i), :] = zout_s[c, i, me_z]
        return copies

    def send_states(c, i, copies):
        arrive(copies)
        part = pl.ds(i * DIM, DIM)
        state = zback_s[c, part, :]
        for place in x_order(c):
            xout_s[c, place, part, :] = state
            state = decay_x(place, i) * state + xin_s[c, place, part, :]
        at = x_at(c, 1, i)
        copies = exchange(
            nx,
            lambda o: xout_s.at[c, x_peer(o), part],
            state_s.at[c, local_part(me_x, i)],
            x_send.at[at],
            x_recv.at[at],
            x_id,
        )
        state_s[c, local_part(me_x, i), :] = xout_s[c, me_x, part, :]
        return copies

    pieces = range(quarter)
    x_copies, dec_copies = [], None
    for i in pieces:
        for h in piece_heads(i):
            prepare(h)
        if i == 0:
            pl.semaphore_wait(barrier, len(peers))
            dec_copies = exchange(
                nx, lambda o: dec_own, dec_x.at[me_x], x_send.at[0], x_recv.at[0], x_id
            )
        x_copies.append(send_local(0, i))

    arrive(dec_copies)
    total_decay = dec_x[0]
    for place in range(1, nx):
        total_decay = total_decay * dec_x[place]
    dec_tot[...] = total_decay
    dec_copies = exchange(nz, lambda o: dec_tot, dec_z.at[me_z], z_send.at[0], z_recv.at[0], z_id)
    dec_z[me_z] = total_decay
    z_copies = [send_total(0, i, x_copies[i]) for i in pieces]

    for h in range(heads):
        gone = jnp.broadcast_to(cumulative[:, h : h + 1], (rows, DIM))
        gap = jnp.where(causal, gone - cumulative_across[h : h + 1, :], 0.0)
        within = jnp.where(causal, jnp.exp(gap), 0.0)
        within_s[h] = within
        scores = dot(q_ref[:, lanes(h)], k_ref[:, lanes(h)], 1, 1)
        weights = (scores * within).astype(BF16)
        weights_s[h] = weights
        mixed_s[h] = dot(weights, v_ref[:, lanes(h)])

    arrive(dec_copies)
    z_copies = [send_scanned(0, i, z_copies[i]) for i in pieces]
    x_copies = [send_states(0, i, z_copies[i]) for i in pieces]
    squares = jnp.zeros((rows, DIM), F32)
    crosses = jnp.zeros((rows, DIM), F32)
    for i in pieces:
        arrive(x_copies[i])
        for h in piece_heads(i):
            low = state_s[0, lanes(h), :].astype(BF16)
            low_s[h] = low
            mixed = mixed_s[h] + cin_s[h] * dot(q_ref[:, lanes(h)], low)
            mixed_s[h] = mixed
            squares = squares + mixed * mixed
            crosses = crosses + g_ref[:, lanes(h)].astype(F32) * mixed

    def as_row(total):
        column = jnp.broadcast_to(jnp.sum(total, axis=1, keepdims=True), (rows, rows))
        return jnp.sum(jnp.where(eye, column, 0.0), axis=0, keepdims=True)

    def as_column(row):
        spread = jnp.where(eye, jnp.broadcast_to(row, (rows, rows)), 0.0)
        return jnp.broadcast_to(jnp.sum(spread, axis=1, keepdims=True), (rows, DIM))

    stat_own[...] = jnp.zeros_like(stat_own)
    stat_own[0:1, :] = as_row(squares)
    stat_own[1:2, :] = as_row(crosses)
    copies = exchange(nh, lambda o: stat_own, stat_in.at[me_h], h_send, h_recv, h_id)
    stat_in[me_h] = stat_own[...]
    arrive(copies)
    totals = stat_in[0]
    for place in range(1, nh):
        totals = totals + stat_in[place]
    inv_row = lax.rsqrt(totals[0:1, :] / feature_total + epsilon)
    inv = as_column(inv_row)
    pull = as_column(inv_row * (inv_row * totals[1:2, :]) / feature_total)

    x_copies = []
    for i in pieces:
        for h in piece_heads(i):
            grad = g_ref[:, lanes(h)].astype(F32)
            d_out = (inv * (grad - mixed_s[h] * pull)).astype(BF16)
            d_s[h] = d_out
            wq = (q_ref[:, lanes(h)].astype(F32) * cin_s[h]).astype(BF16)
            local_s[1, lanes(h), :] = dot(wq, d_out, 0, 0)
        x_copies.append(send_local(1, i))

    def scores_back(h):
        d_out = d_s[h]
        mixed_s[h] = dot(weights_s[h], d_out, 0, 0)
        score_grad = (dot(d_out, v_ref[:, lanes(h)], 1, 1) * within_s[h]).astype(BF16)
        kg_s[h] = dot(score_grad, q_ref[:, lanes(h)], 0, 0)
        carried = cin_s[h] * dot(d_out, low_s[h], 1, 1)
        dq_ref[:, lanes(h)] = (dot(score_grad, k_ref[:, lanes(h)]) + carried).astype(BF16)

    z_copies = [send_total(1, i, x_copies[i]) for i in pieces]
    for h in range(heads):
        scores_back(h)
    z_copies = [send_scanned(1, i, z_copies[i]) for i in pieces]
    x_copies = [send_states(1, i, z_copies[i]) for i in pieces]
    for i in pieces:
        arrive(x_copies[i])
        for h in piece_heads(i):
            later = state_s[1, lanes(h), :].astype(BF16)
            key_grad = kg_s[h] + end_s[h] * dot(v_ref[:, lanes(h)], later, 1, 1)
            dk_ref[:, lanes(h)] = key_grad.astype(BF16)
            value_grad = mixed_s[h] + dot(wk_s[h], later)
            dv_ref[:, lanes(h)] = value_grad.astype(BF16)
    for copy in waits:
        copy.wait_send()


def hand_on(a_ref, b_ref, c_ref, a_out, b_out, c_out, held, in_sem, out_sem):
    reads = [
        pltpu.make_async_copy(ref, held.at[n], in_sem.at[n])
        for n, ref in enumerate((a_ref, b_ref, c_ref))
    ]
    writes = [
        pltpu.make_async_copy(held.at[n], ref, out_sem.at[n])
        for n, ref in enumerate((a_out, b_out, c_out))
    ]
    for read in reads:
        read.start()
    for read, write in zip(reads, writes):
        read.wait()
        write.start()
    for write in writes:
        write.wait()


def local(nx, nz, nh, queries, key_rows, value_rows, log_decay, doc_start, out_cotangent):
    rows, width = queries.shape
    heads = width // DIM
    quarter = heads // nx * DIM
    chunk = DIM // nz
    pieces = quarter // DIM
    slots = 1 + 4 * pieces
    vmem = pl.BlockSpec(memory_space=pltpu.VMEM)
    smem = pl.BlockSpec(memory_space=pltpu.SMEM)
    square = pltpu.VMEM((heads, rows, DIM), F32)
    square_low = pltpu.VMEM((heads, rows, DIM), BF16)
    out = jax.ShapeDtypeStruct((rows, width), BF16)
    grads = pl.pallas_call(
        functools.partial(kernel, nx, nz, nh),
        out_shape=(out, out, out),
        in_specs=[vmem, vmem, vmem, vmem, smem, vmem],
        out_specs=(vmem, vmem, vmem),
        scratch_shapes=[
            square,
            square,
            square,
            square_low,
            square_low,
            square_low,
            square,
            square,
            pltpu.VMEM((heads, DIM, DIM), BF16),
            pltpu.VMEM((heads, DIM), F32),
            pltpu.VMEM((nx, heads, DIM), F32),
            pltpu.VMEM((heads, DIM), F32),
            pltpu.VMEM((nz, heads, DIM), F32),
            pltpu.VMEM((2, heads * DIM, DIM), F32),
            pltpu.VMEM((2, nx, quarter, DIM), F32),
            pltpu.VMEM((2, quarter, DIM), F32),
            pltpu.VMEM((2, pieces, nz, chunk, DIM), F32),
            pltpu.VMEM((2, pieces, nz, chunk, DIM), F32),
            pltpu.VMEM((2, quarter, DIM), F32),
            pltpu.VMEM((2, nx, quarter, DIM), F32),
            pltpu.VMEM((2, heads * DIM, DIM), F32),
            pltpu.VMEM((8, DIM), F32),
            pltpu.VMEM((nh, 8, DIM), F32),
            pltpu.SemaphoreType.DMA((slots, nx)),
            pltpu.SemaphoreType.DMA((slots, nx)),
            pltpu.SemaphoreType.DMA((slots, nz)),
            pltpu.SemaphoreType.DMA((slots, nz)),
            pltpu.SemaphoreType.DMA((nh,)),
            pltpu.SemaphoreType.DMA((nh,)),
        ],
        compiler_params=pltpu.CompilerParams(collective_id=0, has_side_effects=True),
    )(queries, key_rows, value_rows, log_decay.T, doc_start, out_cotangent)
    anywhere = pl.BlockSpec(memory_space=pl.ANY)
    return pl.pallas_call(
        hand_on,
        out_shape=(out, out, out),
        in_specs=[anywhere] * 3,
        out_specs=(anywhere,) * 3,
        scratch_shapes=[
            pltpu.VMEM((3, rows, width), BF16),
            pltpu.SemaphoreType.DMA((3,)),
            pltpu.SemaphoreType.DMA((3,)),
        ],
    )(*grads)


def solution(mesh):
    nx = X_SIZE
    nz, nh = mesh.shape["ctx"] // nx, mesh.shape["head"]
    wide = P("ctx", "head")
    return jax.shard_map(
        functools.partial(local, nx, nz, nh),
        mesh=mesh,
        in_specs=(wide, wide, wide, wide, P("ctx"), wide),
        out_specs=(wide, wide, wide),
        check_vma=False,
    )
```

```python
import functools

import jax
import jax.numpy as jnp
from jax import lax
from jax.experimental import pallas as pl
from jax.experimental.pallas import tpu as pltpu
from jax.sharding import PartitionSpec as P

epsilon = 1e-05
DIM = 128
X_SIZE = 4
BF16, F32 = jnp.bfloat16, jnp.float32
HIGHEST = lax.Precision.HIGHEST


def dot(left, right, left_dim=1, right_dim=0, precision=None):
    return lax.dot_general(
        left,
        right,
        (((left_dim,), (right_dim,)), ((), ())),
        precision=precision,
        preferred_element_type=F32,
    )


def kernel(
    nx,
    nz,
    nh,
    q_hbm,
    k_hbm,
    v_hbm,
    decay_hbm,
    doc_ref,
    g_hbm,
    dq_ref,
    dk_ref,
    dv_ref,
    within_s,
    cin_s,
    end_s,
    weights_s,
    wk_s,
    d_s,
    mixed_s,
    kg_s,
    low_s,
    dec_own,
    dec_x,
    dec_tot,
    dec_z,
    local_s,
    xin_s,
    tot_s,
    zin_s,
    zout_s,
    zback_s,
    xout_s,
    state_s,
    stat_own,
    stat_in,
    x_send,
    x_recv,
    z_send,
    z_recv,
    h_send,
    h_recv,
    wide_s,
    decay_ref,
    in_sem,
):
    q_ref, k_ref, v_ref, g_ref = (wide_s.at[n] for n in range(4))
    rows = q_ref.shape[0]
    heads = q_ref.shape[1] // DIM
    quarter = heads // nx
    qrows = quarter * DIM
    chunk = DIM // nz
    feature_total = heads * DIM * nh
    ctx, me_h = lax.axis_index("ctx"), lax.axis_index("head")
    me_z, me_x = ctx // nx, ctx % nx
    waits = []

    def x_peer(o):
        return lax.rem(me_x + o, nx)

    def z_peer(o):
        return lax.rem(me_z + o, nz)

    def h_peer(o):
        return lax.rem(me_h + o, nh)

    def x_id(o):
        return {"ctx": me_z * nx + x_peer(o)}

    def z_id(o):
        return {"ctx": z_peer(o) * nx + me_x}

    def h_id(o):
        return {"head": h_peer(o)}

    def exchange(count, source, target, send, recv, device):
        copies = []
        for o in sorted(range(1, count), key=lambda o: -min(o, count - o)):
            copy = pltpu.make_async_remote_copy(
                src_ref=source(o),
                dst_ref=target,
                send_sem=send.at[o],
                recv_sem=recv.at[o],
                device_id=device(o),
                device_id_type=pl.DeviceIdType.MESH,
            )
            copy.start()
            copies.append(copy)
        waits.extend(copies)
        return copies

    def arrive(copies):
        for copy in copies:
            copy.wait_recv()

    def lanes(h):
        return pl.ds(h * DIM, DIM)

    barrier = pltpu.get_barrier_semaphore()
    peers = [z_id(o) for o in sorted(range(1, nz), key=lambda o: -min(o, nz - o))]
    peers += [x_id(o) for o in range(1, nx)]
    peers += [h_id(o) for o in range(1, nh)]
    for peer in peers:
        pl.semaphore_signal(barrier, inc=1, device_id=peer, device_id_type=pl.DeviceIdType.MESH)

    loads = [
        pltpu.make_async_copy(source, target, in_sem.at[n])
        for n, (source, target) in enumerate(
            (
                (decay_hbm, decay_ref),
                (k_hbm, k_ref),
                (v_hbm, v_ref),
                (q_hbm, q_ref),
                (g_hbm, g_ref),
            )
        )
    ]
    for load in loads:
        load.start()
    for load in loads:
        load.wait()

    down = lax.broadcasted_iota(jnp.int32, (rows, rows), 0)
    across = lax.broadcasted_iota(jnp.int32, (rows, rows), 1)
    eye = down == across
    lower = down >= across
    blocks = doc_ref.shape[0]
    size = rows // blocks
    reset_down = jnp.zeros((rows, rows), F32)
    reset_across = jnp.zeros((rows, rows), F32)
    for b in range(blocks):
        at = jnp.where(doc_ref[b] < size, b * size + doc_ref[b], -1)
        reset_down = reset_down + jnp.where(down == at, 1.0, 0.0)
        reset_across = reset_across + jnp.where(across == at, 1.0, 0.0)
    ones_lower = jnp.where(lower, 1.0, 0.0)
    ones_upper = jnp.where(down <= across, 1.0, 0.0)
    segment = dot(ones_lower, reset_down)
    segment_across = dot(reset_across, ones_upper)
    causal = lower & (segment == segment_across)
    decays = decay_ref[...]
    cumulative = dot(ones_lower, decays, 1, 1, precision=HIGHEST)
    cumulative_across = dot(decays, ones_upper, precision=HIGHEST)
    first = segment == 0.0
    to_last = segment == segment[rows - 1 : rows, :]
    span_end = jnp.broadcast_to(cumulative_across[:, rows - 1 : rows], (heads, DIM))
    dec_own[...] = jnp.where(first[rows - 1 : rows, :], jnp.exp(span_end), 0.0)
    dec_x[me_x] = dec_own[...]

    def prepare(h):
        gone = jnp.broadcast_to(cumulative[:, h : h + 1], (rows, DIM))
        cin_s[h] = jnp.where(first, jnp.exp(gone), 0.0)
        to_end = jnp.where(to_last, jnp.exp(gone[rows - 1 : rows, :] - gone), 0.0)
        end_s[h] = to_end
        wk = (k_ref[:, lanes(h)].astype(F32) * to_end).astype(BF16)
        wk_s[h] = wk
        local_s[0, lanes(h), :] = dot(wk, v_ref[:, lanes(h)], 0, 0)

    def piece_heads(i):
        return [j * quarter + i for j in range(nx)]

    def x_at(c, back, i):
        return 1 + (c * 2 + back) * quarter + i

    def local_part(place, i):
        return pl.ds(pl.multiple_of(place * qrows + i * DIM, DIM), DIM)

    def chunk_part(place, i):
        return pl.ds(pl.multiple_of(i * DIM + place * chunk, chunk), chunk)

    def x_order(c):
        return range(nx) if c == 0 else range(nx - 1, -1, -1)

    def decay_x(place, i):
        return dec_x[place, pl.ds(me_x * quarter + i, 1), :]

    def send_local(c, i):
        at = x_at(c, 0, i)
        copies = exchange(
            nx,
            lambda o: local_s.at[c, local_part(x_peer(o), i)],
            xin_s.at[c, me_x, pl.ds(i * DIM, DIM)],
            x_send.at[at],
            x_recv.at[at],
            x_id,
        )
        xin_s[c, me_x, pl.ds(i * DIM, DIM), :] = local_s[c, local_part(me_x, i), :]
        return copies

    def send_total(c, i, copies):
        arrive(copies)
        part = pl.ds(i * DIM, DIM)
        total = None
        for place in x_order(c):
            term = xin_s[c, place, part, :]
            total = term if total is None else decay_x(place, i) * total + term
        tot_s[c, part, :] = total
        at = x_at(c, 0, i)
        copies = exchange(
            nz,
            lambda o: tot_s.at[c, chunk_part(z_peer(o), i)],
            zin_s.at[c, i, me_z],
            z_send.at[at],
            z_recv.at[at],
            z_id,
        )
        zin_s[c, i, me_z] = tot_s[c, chunk_part(me_z, i), :]
        return copies

    def send_scanned(c, i, copies):
        arrive(copies)
        state = jnp.zeros((chunk, DIM), F32)
        for place in range(nz) if c == 0 else range(nz - 1, -1, -1):
            zout_s[c, i, place] = state
            decay = dec_z[place, i : i + 1, :]
            state = decay * state + zin_s[c, i, place]
        at = x_at(c, 1, i)
        copies = exchange(
            nz,
            lambda o: zout_s.at[c, i, z_peer(o)],
            zback_s.at[c, chunk_part(me_z, i)],
            z_send.at[at],
            z_recv.at[at],
            z_id,
        )
        zback_s[c, chunk_part(me_z, i), :] = zout_s[c, i, me_z]
        return copies

    def send_states(c, i, copies):
        arrive(copies)
        part = pl.ds(i * DIM, DIM)
        state = zback_s[c, part, :]
        for place in x_order(c):
            xout_s[c, place, part, :] = state
            state = decay_x(place, i) * state + xin_s[c, place, part, :]
        at = x_at(c, 1, i)
        copies = exchange(
            nx,
            lambda o: xout_s.at[c, x_peer(o), part],
            state_s.at[c, local_part(me_x, i)],
            x_send.at[at],
            x_recv.at[at],
            x_id,
        )
        state_s[c, local_part(me_x, i), :] = xout_s[c, me_x, part, :]
        return copies

    pieces = range(quarter)
    for i in pieces:
        for h in piece_heads(i):
            prepare(h)
    for h in range(heads):
        gone = jnp.broadcast_to(cumulative[:, h : h + 1], (rows, DIM))
        gap = jnp.where(causal, gone - cumulative_across[h : h + 1, :], 0.0)
        within = jnp.where(causal, jnp.exp(gap), 0.0)
        within_s[h] = within
        scores = dot(q_ref[:, lanes(h)], k_ref[:, lanes(h)], 1, 1)
        weights = (scores * within).astype(BF16)
        weights_s[h] = weights
        mixed_s[h] = dot(weights, v_ref[:, lanes(h)])

    x_copies, dec_copies = [], None
    for i in pieces:
        if i == 0:
            pl.semaphore_wait(barrier, len(peers))
            dec_copies = exchange(
                nx, lambda o: dec_own, dec_x.at[me_x], x_send.at[0], x_recv.at[0], x_id
            )
        x_copies.append(send_local(0, i))

    arrive(dec_copies)
    for i in range(quarter):
        total_decay = decay_x(0, i)
        for place in range(1, nx):
            total_decay = total_decay * decay_x(place, i)
        dec_tot[i : i + 1, :] = total_decay
    dec_copies = exchange(nz, lambda o: dec_tot, dec_z.at[me_z], z_send.at[0], z_recv.at[0], z_id)
    dec_z[me_z] = dec_tot[...]
    z_copies = [send_total(0, i, x_copies[i]) for i in pieces]

    arrive(dec_copies)
    z_copies = [send_scanned(0, i, z_copies[i]) for i in pieces]
    x_copies = [send_states(0, i, z_copies[i]) for i in pieces]
    squares = jnp.zeros((rows, DIM), F32)
    crosses = jnp.zeros((rows, DIM), F32)
    for i in pieces:
        arrive(x_copies[i])
        for h in piece_heads(i):
            low = state_s[0, lanes(h), :].astype(BF16)
            low_s[h] = low
            mixed = mixed_s[h] + cin_s[h] * dot(q_ref[:, lanes(h)], low)
            mixed_s[h] = mixed
            squares = squares + mixed * mixed
            crosses = crosses + g_ref[:, lanes(h)].astype(F32) * mixed

    def as_row(total):
        column = jnp.broadcast_to(jnp.sum(total, axis=1, keepdims=True), (rows, rows))
        return jnp.sum(jnp.where(eye, column, 0.0), axis=0, keepdims=True)

    def as_column(row):
        spread = jnp.where(eye, jnp.broadcast_to(row, (rows, rows)), 0.0)
        return jnp.broadcast_to(jnp.sum(spread, axis=1, keepdims=True), (rows, DIM))

    stat_own[...] = jnp.zeros_like(stat_own)
    stat_own[0:1, :] = as_row(squares)
    stat_own[1:2, :] = as_row(crosses)
    copies = exchange(nh, lambda o: stat_own, stat_in.at[me_h], h_send, h_recv, h_id)
    stat_in[me_h] = stat_own[...]
    arrive(copies)
    totals = stat_in[0]
    for place in range(1, nh):
        totals = totals + stat_in[place]
    inv_row = lax.rsqrt(totals[0:1, :] / feature_total + epsilon)
    inv = as_column(inv_row)
    pull = as_column(inv_row * (inv_row * totals[1:2, :]) / feature_total)

    x_copies = []
    for i in pieces:
        for h in piece_heads(i):
            grad = g_ref[:, lanes(h)].astype(F32)
            d_out = (inv * (grad - mixed_s[h] * pull)).astype(BF16)
            d_s[h] = d_out
            wq = (q_ref[:, lanes(h)].astype(F32) * cin_s[h]).astype(BF16)
            local_s[1, lanes(h), :] = dot(wq, d_out, 0, 0)
        x_copies.append(send_local(1, i))

    def scores_back(h):
        d_out = d_s[h]
        mixed_s[h] = dot(weights_s[h], d_out, 0, 0)
        score_grad = (dot(d_out, v_ref[:, lanes(h)], 1, 1) * within_s[h]).astype(BF16)
        kg_s[h] = dot(score_grad, q_ref[:, lanes(h)], 0, 0)
        carried = cin_s[h] * dot(d_out, low_s[h], 1, 1)
        dq_ref[:, lanes(h)] = (dot(score_grad, k_ref[:, lanes(h)]) + carried).astype(BF16)

    for h in range(heads // 2):
        scores_back(h)
    z_copies = [send_total(1, i, x_copies[i]) for i in pieces]
    for h in range(heads // 2, heads):
        scores_back(h)
    z_copies = [send_scanned(1, i, z_copies[i]) for i in pieces]
    x_copies = [send_states(1, i, z_copies[i]) for i in pieces]
    for i in pieces:
        arrive(x_copies[i])
        for h in piece_heads(i):
            later = state_s[1, lanes(h), :].astype(BF16)
            key_grad = kg_s[h] + end_s[h] * dot(v_ref[:, lanes(h)], later, 1, 1)
            dk_ref[:, lanes(h)] = key_grad.astype(BF16)
            value_grad = mixed_s[h] + dot(wk_s[h], later)
            dv_ref[:, lanes(h)] = value_grad.astype(BF16)
    for copy in waits:
        copy.wait_send()


def hand_on(a_ref, b_ref, c_ref, a_out, b_out, c_out, held, in_sem, out_sem):
    reads = [
        pltpu.make_async_copy(ref, held.at[n], in_sem.at[n])
        for n, ref in enumerate((a_ref, b_ref, c_ref))
    ]
    writes = [
        pltpu.make_async_copy(held.at[n], ref, out_sem.at[n])
        for n, ref in enumerate((a_out, b_out, c_out))
    ]
    for read in reads:
        read.start()
    for read, write in zip(reads, writes):
        read.wait()
        write.start()
    for write in writes:
        write.wait()


def local(nx, nz, nh, queries, key_rows, value_rows, log_decay, doc_start, out_cotangent):
    rows, width = queries.shape
    heads = width // DIM
    quarter = heads // nx * DIM
    chunk = DIM // nz
    pieces = quarter // DIM
    slots = 1 + 4 * pieces
    vmem = pl.BlockSpec(memory_space=pltpu.VMEM)
    smem = pl.BlockSpec(memory_space=pltpu.SMEM)
    anywhere = pl.BlockSpec(memory_space=pl.ANY)
    square = pltpu.VMEM((heads, rows, DIM), F32)
    square_low = pltpu.VMEM((heads, rows, DIM), BF16)
    out = jax.ShapeDtypeStruct((rows, width), BF16)
    grads = pl.pallas_call(
        functools.partial(kernel, nx, nz, nh),
        out_shape=(out, out, out),
        in_specs=[anywhere, anywhere, anywhere, anywhere, smem, anywhere],
        out_specs=(vmem, vmem, vmem),
        scratch_shapes=[
            square,
            square,
            square,
            square_low,
            square_low,
            square_low,
            square,
            square,
            pltpu.VMEM((heads, DIM, DIM), BF16),
            pltpu.VMEM((heads, DIM), F32),
            pltpu.VMEM((nx, heads, DIM), F32),
            pltpu.VMEM((pieces, DIM), F32),
            pltpu.VMEM((nz, pieces, DIM), F32),
            pltpu.VMEM((2, heads * DIM, DIM), F32),
            pltpu.VMEM((2, nx, quarter, DIM), F32),
            pltpu.VMEM((2, quarter, DIM), F32),
            pltpu.VMEM((2, pieces, nz, chunk, DIM), F32),
            pltpu.VMEM((2, pieces, nz, chunk, DIM), F32),
            pltpu.VMEM((2, quarter, DIM), F32),
            pltpu.VMEM((2, nx, quarter, DIM), F32),
            pltpu.VMEM((2, heads * DIM, DIM), F32),
            pltpu.VMEM((8, DIM), F32),
            pltpu.VMEM((nh, 8, DIM), F32),
            pltpu.SemaphoreType.DMA((slots, nx)),
            pltpu.SemaphoreType.DMA((slots, nx)),
            pltpu.SemaphoreType.DMA((slots, nz)),
            pltpu.SemaphoreType.DMA((slots, nz)),
            pltpu.SemaphoreType.DMA((nh,)),
            pltpu.SemaphoreType.DMA((nh,)),
            pltpu.VMEM((4, rows, width), BF16),
            pltpu.VMEM((heads, rows), F32),
            pltpu.SemaphoreType.DMA((5,)),
        ],
        compiler_params=pltpu.CompilerParams(collective_id=0, has_side_effects=True),
    )(queries, key_rows, value_rows, log_decay.T, doc_start, out_cotangent)
    return pl.pallas_call(
        hand_on,
        out_shape=(out, out, out),
        in_specs=[anywhere] * 3,
        out_specs=(anywhere,) * 3,
        scratch_shapes=[
            pltpu.VMEM((3, rows, width), BF16),
            pltpu.SemaphoreType.DMA((3,)),
            pltpu.SemaphoreType.DMA((3,)),
        ],
    )(*grads)


def solution(mesh):
    nx = X_SIZE
    nz, nh = mesh.shape["ctx"] // nx, mesh.shape["head"]
    wide = P("ctx", "head")
    return jax.shard_map(
        functools.partial(local, nx, nz, nh),
        mesh=mesh,
        in_specs=(wide, wide, wide, wide, P("ctx"), wide),
        out_specs=(wide, wide, wide),
        check_vma=False,
    )
```
